32 devices in a mesh: dp: 16 (over z, x, core), tensor: 2 (over y).
Axes of the slice: x: 2, y: 2, z: 4, core: 2. Of those that a mesh axis runs over, the one named last changes fastest.
Arguments:
- tokens: bfloat16 [16384, 1024], P(('dp', 'tensor')), may hold values from -6 to 6
- cotangent: bfloat16 [16384, 1024], P(('dp', 'tensor')), may hold values from -6 to 6
- gain_one: float32 [1024], replicated, may hold values from 0.1 to 1.9
- bias_one: float32 [1024], replicated, may hold values from -3 to 3
- w_qkv: bfloat16 [1024, 3, 1024], P(None, None, 'tensor'), may hold values from -0.1875 to 0.1875
- bias_qv: float32 [2, 1024], P(None, 'tensor'), may hold values from -3 to 3
- w_out: bfloat16 [1024, 1024], P('tensor'), may hold values from -3 to 3
- out_bias: float32 [1024], replicated, may hold values from -4 to 4
- gain_two: float32 [1024], replicated, may hold values from 0.1 to 1.9
- bias_two: float32 [1024], replicated, may hold values from -3 to 3
- w_fc: bfloat16 [1024, 4096], P(None, 'tensor'), may hold values from -0.1875 to 0.1875
- fc_bias: float32 [4096], P('tensor'), may hold values from -3 to 3
- w_proj: bfloat16 [4096, 1024], P('tensor'), may hold values from -0.5 to 0.5
- proj_bias: float32 [1024], replicated, may hold values from -4 to 4
Outputs:
- block_out: bfloat16 [2, 16384, 1024], P(None, ('dp', 'tensor'))
- grad_tokens: float32 [2, 16384, 1024], P(None, ('dp', 'tensor'))
- grad_gain_one: float32 [2, 1024], replicated
- grad_bias_one: float32 [2, 1024], replicated
- grad_w_qkv: float32 [2, 1024, 3, 1024], P(None, None, None, 'tensor')
- grad_bias_qv: float32 [2, 2, 1024], P(None, None, 'tensor')
- grad_w_out: float32 [2, 1024, 1024], P(None, 'tensor')
- grad_out_bias: float32 [2, 1024], replicated
- grad_gain_two: float32 [2, 1024], replicated
- grad_bias_two: float32 [2, 1024], replicated
- grad_w_fc: float32 [2, 1024, 4096], P(None, None, 'tensor')
- grad_fc_bias: float32 [2, 4096], P(None, 'tensor')
- grad_w_proj: float32 [2, 4096, 1024], P(None, 'tensor')
- grad_proj_bias: float32 [2, 1024], replicated
The draws below stay inside these ranges and needn't reach their ends.
All inputs are finite; a program needn't handle non-finite values.
Results may differ from the reference program's by a relative error of at most 0.012.
The reference program's roundings to bfloat16 on the way count: a program that leaves them out, or rounds other values in their place, can miss the bound.
Values may be sent and summed in bfloat16 or wider, within the bound.
No kernel may reach another device: no remote copies, remote signals or barrier semaphores. Data moves between devices by JAX's collectives and lax.ppermute only.
A program may use at most 320 MiB of HBM per device.

```python
import jax
import jax.numpy as jnp
from jax import lax

D = 1024
HEAD = 64
FF = 4096
LEN = 1024
DEPTH_A = 12
DEPTH_B = 48
TOKENS = 16384


def shard_levels(rng, extent, cuts, low, high):
    gain, own = 1.0, jax.random.fold_in(rng, 6)
    for dim, parts in cuts:
        steps = jnp.exp(jax.random.uniform(jax.random.fold_in(own, dim), (parts,), jnp.float32, low / len(cuts), high / len(cuts)))
        gain = gain * jnp.repeat(steps, extent[dim] // parts).reshape([-1 if axis == dim else 1 for axis in range(len(extent))])
    return gain


def scatter_about(key, dims, width, most, cuts=(), kind=jnp.bfloat16):
    entries = width * jax.random.normal(key, dims, jnp.float32)
    if cuts:
        entries = entries * shard_levels(key, dims, cuts, -0.22, 0.18)
    return jnp.clip(entries, -most, most).astype(kind)


def setup_inputs(seed: int = 0) -> dict:
    key_list = jax.random.split(jax.random.key(seed), 15)
    tokens = scatter_about(key_list[0], (TOKENS, D), 1.0, 6.0, ((0, 32),))
    cotangent = scatter_about(key_list[1], (TOKENS, D), 1.0, 6.0, ((0, 32),))
    gain_one = jnp.clip(1.0 + 0.18 * jax.random.normal(key_list[2], (D,), jnp.float32), 0.1, 1.9)
    bias_one = scatter_about(key_list[3], (D,), 0.5, 3.0, (), jnp.float32)
    w_qkv = scatter_about(key_list[4], (D, 3, D), D ** -0.5, 0.1875, ((2, 2),))
    bias_qv = scatter_about(key_list[5], (2, D), 0.5, 3.0, ((1, 2),), jnp.float32)
    w_out = scatter_about(key_list[6], (D, D), (max(D * 4 // LEN, 4)) ** -0.5, 3.0, ((0, 2),))
    out_bias = scatter_about(key_list[7], (D,), 1.0, 4.0, (), jnp.float32)
    gain_two = jnp.clip(1.0 + 0.18 * jax.random.normal(key_list[8], (D,), jnp.float32), 0.1, 1.9)
    bias_two = scatter_about(key_list[9], (D,), 0.5, 3.0, (), jnp.float32)
    w_fc = scatter_about(key_list[10], (D, FF), D ** -0.5, 0.1875, ((1, 2),))
    fc_bias = scatter_about(key_list[11], (FF,), 0.5, 3.0, ((0, 2),), jnp.float32)
    w_proj = scatter_about(key_list[12], (FF, D), (FF // 32) ** -0.5, 0.5, ((0, 2),))
    proj_bias = scatter_about(key_list[13], (D,), 1.0, 4.0, (), jnp.float32)
    return {"tokens": tokens, "cotangent": cotangent, "gain_one": gain_one, "bias_one": bias_one, "w_qkv": w_qkv, "bias_qv": bias_qv, "w_out": w_out, "out_bias": out_bias, "gain_two": gain_two, "bias_two": bias_two, "w_fc": w_fc, "fc_bias": fc_bias, "w_proj": w_proj, "proj_bias": proj_bias}


@jax.custom_vjp
def low(v):
    return lax.optimization_barrier(v.astype(jnp.bfloat16)).astype(jnp.float32)

@jax.custom_vjp
def low_back(v):
    return v

def low_keep(v):
    return (low(v), None)

def low_pass(kept, grad):
    return (grad,)

def back_keep(v):
    return (v, None)

def back_low(kept, grad):
    return (low(grad),)
low.defvjp(low_keep, low_pass)
low_back.defvjp(back_keep, back_low)
precise = lax.Precision.HIGHEST

def norm_layer(values, norm_gain, norm_bias):
    centre = values - lax.optimization_barrier(jnp.mean(values, axis=-1, keepdims=True))
    spread = lax.optimization_barrier(jnp.mean(centre * centre, axis=-1, keepdims=True))
    return centre * lax.rsqrt(spread + 1e-05) * norm_gain + norm_bias

def attention(queries, key_rows, value_rows):
    length = queries.shape[0]
    block_rows = min(512, length)
    block_count = length // block_rows
    blocks = queries.reshape(block_count, block_rows, queries.shape[1], queries.shape[2])
    starts = jnp.arange(block_count, dtype=jnp.int32) * block_rows

    def one_block(packed):
        query_rows, offset = packed
        scores = low_back(0.125 * jnp.einsum('qhe,khe->hqk', query_rows, key_rows, precision=precise))
        query_pos = offset + jnp.arange(block_rows, dtype=jnp.int32)
        key_pos = jnp.arange(length, dtype=jnp.int32)
        allowed = key_pos[None, :] <= query_pos[:, None]
        scores = jnp.where(allowed[None], scores, -1e+30)
        highest = lax.optimization_barrier(jnp.max(scores, axis=-1, keepdims=True))
        raised = jnp.exp(scores - highest)
        probabilities = low(raised / lax.optimization_barrier(jnp.sum(raised, axis=-1, keepdims=True)))
        return jnp.einsum('hqk,khe->qhe', probabilities, value_rows, precision=precise)
    mixed = lax.map(jax.checkpoint(one_block), (blocks, starts))
    return mixed.reshape(length, -1)

def block_forward(inputs, weights_all, branch_scale):
    gain_one, bias_one, w_qkv, bias_qv, w_out, out_bias, gain_two, bias_two, w_fc, fc_bias, w_proj, proj_bias = weights_all
    normed = low(norm_layer(inputs, gain_one, bias_one))
    projected = jnp.einsum('td,dcf->tcf', normed, w_qkv, precision=precise)
    queries = low(low_back(projected[:, 0] + bias_qv[0]))
    key_rows = low(low_back(projected[:, 1]))
    value_rows = low(low_back(projected[:, 2] + bias_qv[1]))
    length = inputs.shape[0]
    mixed = attention(queries.reshape(length, -1, HEAD), key_rows.reshape(length, -1, HEAD), value_rows.reshape(length, -1, HEAD))
    mixed = low(low_back(mixed))
    branch = low_back(jnp.dot(mixed, w_out, precision=precise, preferred_element_type=jnp.float32) + out_bias)
    middle = inputs + branch_scale * branch
    normed_two = low(norm_layer(middle, gain_two, bias_two))
    hidden = low_back(jnp.dot(normed_two, w_fc, precision=precise, preferred_element_type=jnp.float32) + fc_bias)
    active = low(jax.nn.gelu(hidden, approximate=True))
    second = low_back(jnp.dot(active, w_proj, precision=precise, preferred_element_type=jnp.float32) + proj_bias)
    return middle + branch_scale * second

def reference(tokens, cotangent, gain_one, bias_one, w_qkv, bias_qv, w_out, out_bias, gain_two, bias_two, w_fc, fc_bias, w_proj, proj_bias):
    weights_all = tuple((item.astype(jnp.float32) for item in (gain_one, bias_one, w_qkv, bias_qv, w_out, out_bias, gain_two, bias_two, w_fc, fc_bias, w_proj, proj_bias)))
    seq_count = tokens.shape[0] // LEN
    inputs = tokens.astype(jnp.float32).reshape(seq_count, LEN, D)
    upstream = cotangent.astype(jnp.float32).reshape(seq_count, LEN, D)
    collected = []
    for depth_count in (DEPTH_A, DEPTH_B):
        branch_scale = float(depth_count) ** (-0.5)

        def apply_block(seq_in, *weight_list):
            return block_forward(seq_in, weight_list, branch_scale)

        def one_sequence(totals, packed):
            seq_in, seq_grad = packed
            result, pullback = jax.vjp(apply_block, seq_in, *weights_all)
            pulled = pullback(seq_grad)
            totals = tuple((left + right for left, right in zip(totals, pulled[1:])))
            return (totals, (result, pulled[0]))
        zeros_all = tuple((jnp.zeros_like(item) for item in weights_all))
        totals, (results, input_grads) = lax.scan(one_sequence, zeros_all, (inputs, upstream))
        collected.append((results.reshape(-1, D).astype(jnp.bfloat16), input_grads.reshape(-1, D), totals))
    stacked = [jnp.stack([entry[0] for entry in collected]), jnp.stack([entry[1] for entry in collected])]
    for index in range(12):
        stacked.append(jnp.stack([entry[2][index] for entry in collected]))
    return (stacked[0], stacked[1], stacked[2], stacked[3], stacked[4], stacked[5], stacked[6], stacked[7], stacked[8], stacked[9], stacked[10], stacked[11], stacked[12], stacked[13])
```

```python
from functools import partial

import jax
import jax.numpy as jnp
from jax import lax
from jax.experimental import pallas as pl
from jax.experimental.pallas import tpu as pltpu
from jax.sharding import PartitionSpec as P

HEAD = 64
LEN = 1024
DEPTH_A = 12
DEPTH_B = 48
PAIR = 2 * HEAD
BLOCK_Q = 256
bf16 = jnp.bfloat16
f32 = jnp.float32

DOT_NT = (((1,), (1,)), ((), ()))
DOT_NN = (((1,), (0,)), ((), ()))
DOT_TN = (((0,), (0,)), ((), ()))


def dot(left, right, dims):
    return lax.dot_general(left, right, dims, preferred_element_type=f32)


def head_rows(rows, head):
    lane = lax.broadcasted_iota(jnp.int32, rows.shape, 1)
    return jnp.where((lane // HEAD) == head, rows, jnp.zeros_like(rows))


def scores_of(key_ref, query_rows, lo, hi):
    diag = dot(key_ref[lo:hi, :], query_rows, DOT_NT)
    key_pos = lax.broadcasted_iota(jnp.int32, diag.shape, 0)
    query_pos = lax.broadcasted_iota(jnp.int32, diag.shape, 1)
    diag = jnp.where(key_pos <= query_pos, diag, -1e30)
    if lo == 0:
        return diag
    return jnp.concatenate([dot(key_ref[:lo, :], query_rows, DOT_NT), diag], axis=0)


def attend_forward_kernel(q_ref, k_ref, v_ref, o_ref, lse_ref, vt_ref):
    vt_ref[...] = v_ref[...].astype(f32).T.astype(bf16)
    for index in range(LEN // BLOCK_Q):
        lo, hi = index * BLOCK_Q, (index + 1) * BLOCK_Q
        query_rows = q_ref[lo:hi, :] * jnp.asarray(0.125, bf16)
        mixed = []
        for head in range(2):
            scores = scores_of(k_ref, head_rows(query_rows, head), lo, hi)
            highest = jnp.max(scores, axis=0, keepdims=True)
            raised = jnp.exp(scores - highest)
            totals = jnp.sum(raised, axis=0, keepdims=True)
            probabilities = (raised * (1.0 / totals)).astype(bf16)
            mixed.append(dot(vt_ref[head * HEAD : (head + 1) * HEAD, :hi], probabilities, DOT_NN))
            lse_ref[0, head : head + 1, lo:hi] = highest + jnp.log(totals)
        o_ref[lo:hi, :] = jnp.concatenate(mixed, axis=0).T.astype(bf16)


def attend_backward_kernel(q_ref, k_ref, v_ref, lse_ref, do_ref, dq_ref, dk_ref, dv_ref, kt_ref, dk_acc, dv_acc):
    kt_ref[...] = k_ref[...].astype(f32).T.astype(bf16)
    blocks = LEN // BLOCK_Q
    for index in reversed(range(blocks)):
        lo, hi = index * BLOCK_Q, (index + 1) * BLOCK_Q
        query_rows = q_ref[lo:hi, :] * jnp.asarray(0.125, bf16)
        grad_rows = do_ref[lo:hi, :]
        probs, grads, queries, douts, dqs = [], [], [], [], []
        for head in range(2):
            query_head = head_rows(query_rows, head)
            grad_head = head_rows(grad_rows, head)
            scores = scores_of(k_ref, query_head, lo, hi)
            probabilities = jnp.exp(scores - lse_ref[0, head : head + 1, lo:hi])
            grad_probs = dot(v_ref[:hi, :], grad_head, DOT_NT)
            centre = jnp.sum(probabilities * grad_probs, axis=0, keepdims=True)
            grad_scores = (probabilities * (grad_probs - centre)).astype(bf16)
            dqs.append(dot(kt_ref[head * HEAD : (head + 1) * HEAD, :hi], grad_scores, DOT_NN))
            probs.append(probabilities.astype(bf16))
            grads.append(grad_scores)
            queries.append(query_head)
            douts.append(grad_head)
        dq_ref[lo:hi, :] = (0.125 * jnp.concatenate(dqs, axis=0).T).astype(bf16)
        dk = dot(jnp.concatenate(grads, axis=1), jnp.concatenate(queries, axis=0), DOT_NN)
        dv = dot(jnp.concatenate(probs, axis=1), jnp.concatenate(douts, axis=0), DOT_NN)
        if index == blocks - 1:
            dk_acc[...] = dk
            dv_acc[...] = dv
        else:
            dk_acc[:hi, :] = dk_acc[:hi, :] + dk
            dv_acc[:hi, :] = dv_acc[:hi, :] + dv
    dk_ref[...] = dk_acc[...].astype(bf16)
    dv_ref[...] = dv_acc[...].astype(bf16)


def attend_forward(queries, key_rows, value_rows):
    rows, cols = queries.shape
    seqs, pairs = rows // LEN, cols // PAIR
    spec = pl.BlockSpec((LEN, PAIR), lambda s, p: (s, p))
    return pl.pallas_call(
        attend_forward_kernel,
        grid=(seqs, pairs),
        in_specs=[spec] * 3,
        out_specs=[spec, pl.BlockSpec((1, 2, LEN), lambda s, p: (s * pairs + p, 0, 0))],
        out_shape=[
            jax.ShapeDtypeStruct((rows, cols), bf16),
            jax.ShapeDtypeStruct((seqs * pairs, 2, LEN), f32),
        ],
        scratch_shapes=[pltpu.VMEM((PAIR, LEN), bf16)],
        name="attend_forward",
    )(queries, key_rows, value_rows)


def attend_backward(queries, key_rows, value_rows, log_totals, grad_mixed):
    rows, cols = queries.shape
    seqs, pairs = rows // LEN, cols // PAIR
    spec = pl.BlockSpec((LEN, PAIR), lambda s, p: (s, p))
    lse_spec = pl.BlockSpec((1, 2, LEN), lambda s, p: (s * pairs + p, 0, 0))
    return pl.pallas_call(
        attend_backward_kernel,
        grid=(seqs, pairs),
        in_specs=[spec, spec, spec, lse_spec, spec],
        out_specs=[spec] * 3,
        out_shape=[jax.ShapeDtypeStruct((rows, cols), bf16)] * 3,
        scratch_shapes=[
            pltpu.VMEM((PAIR, LEN), bf16),
            pltpu.VMEM((LEN, PAIR), f32),
            pltpu.VMEM((LEN, PAIR), f32),
        ],
        name="attend_backward",
    )(queries, key_rows, value_rows, log_totals, grad_mixed)


GELU_C = 0.7978845608028654


def hidden_kernel(scale_a, ha_ref, hb_ref, dz_ref, wfc_ref, bias_ref, wproj_ref, fa_ref, fb_ref, dua_ref, dub_ref, sa_ref, sb_ref):
    grad_active = dot(dz_ref[...], wproj_ref[...], DOT_NT)
    for h_ref, f_ref, du_ref, s_ref, scale in (
        (ha_ref, fa_ref, dua_ref, sa_ref, scale_a),
        (hb_ref, fb_ref, dub_ref, sb_ref, 1.0),
    ):
        hidden = dot(h_ref[...], wfc_ref[...], DOT_NN) + bias_ref[...]
        square = hidden * hidden
        bend = jnp.tanh(GELU_C * (hidden + 0.044715 * (hidden * square)))
        cdf = 0.5 * (1.0 + bend)
        f_ref[...] = (hidden * cdf).astype(bf16)
        slope = cdf + hidden * (0.5 * (1.0 - bend * bend)) * (
            GELU_C * (1.0 + (3 * 0.044715) * square)
        )
        grad = ((scale * grad_active) * slope).astype(bf16)
        du_ref[...] = grad
        s_ref[0] = jnp.sum(grad.astype(f32), axis=0, keepdims=True)


def hidden_layer(scale_a, h_a, h_b, dz, w_fc, fc_bias, w_proj):
    rows, width = h_a.shape
    hidden = w_fc.shape[1]
    tile_r = min(512, rows)
    tile_c = min(512, hidden)
    row_spec = pl.BlockSpec((tile_r, width), lambda r, c: (r, 0))
    out_spec = pl.BlockSpec((tile_r, tile_c), lambda r, c: (r, c))
    sum_spec = pl.BlockSpec((1, 1, tile_c), lambda r, c: (r, 0, c))
    out = jax.ShapeDtypeStruct((rows, hidden), bf16)
    sums = jax.ShapeDtypeStruct((rows // tile_r, 1, hidden), f32)
    return pl.pallas_call(
        partial(hidden_kernel, scale_a),
        grid=(rows // tile_r, hidden // tile_c),
        in_specs=[
            row_spec,
            row_spec,
            row_spec,
            pl.BlockSpec((width, tile_c), lambda r, c: (0, c)),
            pl.BlockSpec((1, tile_c), lambda r, c: (0, c)),
            pl.BlockSpec((tile_c, width), lambda r, c: (c, 0)),
        ],
        out_specs=[out_spec] * 4 + [sum_spec] * 2,
        out_shape=[out] * 4 + [sums] * 2,
        name="hidden_layer",
    )(h_a, h_b, dz, w_fc, fc_bias.reshape(1, hidden), w_proj)


def norm_parts(values):
    centre = values - jnp.mean(values, axis=-1, keepdims=True)
    spread = jnp.mean(centre * centre, axis=-1, keepdims=True)
    inverse = lax.rsqrt(spread + 1e-05)
    return centre * inverse, inverse


def norm_back(unit, inverse, gain, grad):
    scaled = grad * gain
    along = jnp.mean(scaled * unit, axis=-1, keepdims=True)
    return inverse * (scaled - jnp.mean(scaled, axis=-1, keepdims=True) - unit * along)


def solution(mesh):
    tensor = mesh.shape["tensor"]
    devices_dp = mesh.shape["dp"]
    swap = [(0, 1), (1, 0)]

    def own_rows(values, rows, other=False):
        place = lax.axis_index("tensor")
        if other:
            place = 1 - place
        return lax.dynamic_slice_in_dim(values, place * rows, rows, axis=0)

    def gather_rows(values):
        if tensor != 2:
            return lax.all_gather(values, "tensor", axis=0, tiled=True)
        there = lax.ppermute(values, "tensor", swap)
        first = lax.axis_index("tensor") == 0
        return jnp.concatenate(
            [jnp.where(first, values, there), jnp.where(first, there, values)], axis=0
        )

    def total_rows(shares):
        if tensor != 2:
            return lax.psum(shares.astype(bf16), "tensor").astype(f32)
        there = lax.ppermute(shares.astype(bf16), "tensor", swap)
        return shares + there.astype(f32)

    def scatter_rows(shares, rows):
        if tensor != 2:
            low = shares.astype(bf16)
            return lax.psum_scatter(low, "tensor", scatter_dimension=0, tiled=True).astype(f32)
        low = shares.astype(bf16)
        there = lax.ppermute(own_rows(low, rows, other=True), "tensor", swap)
        return own_rows(low, rows).astype(f32) + there.astype(f32)

    def reduce_dp(share):
        shape = share.shape
        flat = share.astype(bf16).reshape(shape[0], -1)
        part = lax.psum_scatter(flat, "dp", scatter_dimension=0, tiled=True)
        return lax.all_gather(part, "dp", axis=0, tiled=True).reshape(shape)

    def per_device(
        tokens,
        cotangent,
        gain_one,
        bias_one,
        w_qkv,
        bias_qv,
        w_out,
        out_bias,
        gain_two,
        bias_two,
        w_fc,
        fc_bias,
        w_proj,
        proj_bias,
    ):
        own, width = tokens.shape
        rows = own * tensor
        cols = w_qkv.shape[2]
        hidden_cols = w_fc.shape[1]
        scale_a = float(DEPTH_A) ** (-0.5)
        scale_b = float(DEPTH_B) ** (-0.5)
        factor = 2.0
        assert scale_a == factor * scale_b

        residual = gather_rows(tokens).astype(f32)
        upstream_low = gather_rows(cotangent)
        upstream = upstream_low.astype(f32)
        unit_one, inverse_one = norm_parts(residual)
        normed = (unit_one * gain_one + bias_one).astype(bf16)
        flat_w = w_qkv.reshape(width, 3 * cols)
        projected = dot(normed, flat_w, DOT_NN)
        queries = (projected[:, :cols] + bias_qv[0]).astype(bf16)
        key_rows = projected[:, cols : 2 * cols].astype(bf16)
        value_rows = (projected[:, 2 * cols :] + bias_qv[1]).astype(bf16)
        mixed, log_totals = attend_forward(queries, key_rows, value_rows)
        branch = total_rows(dot(mixed, w_out, DOT_NN)) + out_bias

        dz = (scale_b * upstream).astype(bf16)
        dz_own = (scale_b * cotangent.astype(f32)).astype(bf16)
        proj_sum = jnp.sum(dz_own.astype(f32), axis=0)

        middles, units, inverses, normed_two = [], [], [], []
        for scale in (scale_a, scale_b):
            middle = residual + scale * branch
            unit, inverse = norm_parts(middle)
            middles.append(middle)
            units.append(unit)
            inverses.append(inverse)
            normed_two.append((unit * gain_two + bias_two).astype(bf16))
        f_a, f_b, du_a, du_b, sum_a, sum_b = hidden_layer(
            factor, normed_two[0], normed_two[1], dz, w_fc, fc_bias, w_proj
        )

        outputs, grad_tokens, vectors, weights = [], [], [], []
        place = lax.axis_index("tensor")
        for depth, (scale, active, grad_hidden, hidden_sum, times) in enumerate(
            ((scale_a, f_a, du_a, sum_a, factor), (scale_b, f_b, du_b, sum_b, 1.0))
        ):
            grad_two = total_rows(dot(grad_hidden, w_fc, DOT_NT))
            grad_w_proj = reduce_dp(times * dot(active, dz, DOT_TN))
            grad_w_fc = reduce_dp(dot(normed_two[depth], grad_hidden, DOT_TN))
            second = scatter_rows(dot(active, w_proj, DOT_NN), own) + proj_bias
            outputs.append((own_rows(middles[depth], own) + scale * second).astype(bf16))

            grad_middle = upstream + norm_back(units[depth], inverses[depth], gain_two, grad_two)
            grad_branch = (scale * grad_middle).astype(bf16)
            own_grad_two = own_rows(grad_two, own)
            grad_gain_two = jnp.sum(own_grad_two * own_rows(units[depth], own), axis=0)
            grad_bias_two = jnp.sum(own_grad_two, axis=0)
            grad_out_bias = jnp.sum(own_rows(grad_branch, own).astype(f32), axis=0)

            grad_w_out = reduce_dp(dot(mixed, grad_branch, DOT_TN))
            grad_mixed = dot(grad_branch, w_out, DOT_NT).astype(bf16)
            dq, dk, dv = attend_backward(queries, key_rows, value_rows, log_totals, grad_mixed)
            stacked = jnp.concatenate([dq, dk, dv], axis=1)
            grad_bias_qv = jnp.stack(
                [jnp.sum(dq.astype(f32), axis=0), jnp.sum(dv.astype(f32), axis=0)]
            )
            grad_w_qkv = reduce_dp(dot(normed, stacked, DOT_TN))
            grad_one_share = dot(stacked, flat_w, DOT_NT)
            grad_gain_one = jnp.sum(grad_one_share * unit_one, axis=0)
            grad_bias_one = jnp.sum(grad_one_share, axis=0)
            grad_one = scatter_rows(grad_one_share, own)
            grad_tokens.append(
                own_rows(grad_middle, own)
                + norm_back(
                    own_rows(unit_one, own), own_rows(inverse_one, own), gain_one, grad_one
                )
            )
            weights.append((grad_w_qkv, grad_w_out, grad_w_fc, grad_w_proj))
            slots = jnp.concatenate(
                [jnp.sum(hidden_sum, axis=(0, 1)), grad_bias_qv[0], grad_bias_qv[1]]
            )
            spread_slots = jnp.where(
                jnp.arange(tensor)[:, None] == place, slots[None, :], 0.0
            ).reshape(-1)
            vectors.append(
                jnp.concatenate(
                    [
                        grad_gain_one,
                        grad_bias_one,
                        grad_out_bias,
                        grad_gain_two,
                        grad_bias_two,
                        times * proj_sum,
                        spread_slots,
                    ]
                )
            )

        summed = lax.psum(jnp.stack(vectors), ("dp", "tensor"))
        small = [summed[:, index * width : (index + 1) * width] for index in range(6)]
        slot_len = hidden_cols + 2 * cols
        mine = lax.dynamic_slice_in_dim(summed, 6 * width + place * slot_len, slot_len, axis=1)
        grad_fc_bias = mine[:, :hidden_cols]
        grad_bias_qv = mine[:, hidden_cols:].reshape(2, 2, cols)
        stack = [
            jnp.stack([weights[0][index].astype(f32), weights[1][index].astype(f32)])
            for index in range(4)
        ]
        return (
            jnp.stack(outputs),
            jnp.stack(grad_tokens),
            small[0],
            small[1],
            stack[0].reshape(2, width, 3, cols),
            grad_bias_qv,
            stack[1],
            small[2],
            small[3],
            small[4],
            stack[2],
            grad_fc_bias,
            stack[3],
            small[5],
        )

    return jax.shard_map(
        per_device,
        mesh=mesh,
        in_specs=(
            P(("dp", "tensor"), None),
            P(("dp", "tensor"), None),
            P(),
            P(),
            P(None, None, "tensor"),
            P(None, "tensor"),
            P("tensor", None),
            P(),
            P(),
            P(),
            P(None, "tensor"),
            P("tensor"),
            P("tensor", None),
            P(),
        ),
        out_specs=(
            P(None, ("dp", "tensor"), None),
            P(None, ("dp", "tensor"), None),
            P(),
            P(),
            P(None, None, None, "tensor"),
            P(None, None, "tensor"),
            P(None, "tensor", None),
            P(),
            P(),
            P(),
            P(None, None, "tensor"),
            P(None, "tensor"),
            P(None, "tensor", None),
            P(),
        ),
        check_vma=False,
    )
```

```python
from functools import partial

import jax
import jax.numpy as jnp
from jax import lax
from jax.experimental import pallas as pl
from jax.experimental.pallas import tpu as pltpu
from jax.sharding import PartitionSpec as P

HEAD = 64
LEN = 1024
DEPTH_A = 12
DEPTH_B = 48
PAIR = 2 * HEAD
BLOCK_Q = 256
bf16 = jnp.bfloat16
f32 = jnp.float32

DOT_NT = (((1,), (1,)), ((), ()))
DOT_NN = (((1,), (0,)), ((), ()))
DOT_TN = (((0,), (0,)), ((), ()))


def dot(left, right, dims):
    return lax.dot_general(left, right, dims, preferred_element_type=f32)


def head_rows(rows, head):
    lane = lax.broadcasted_iota(jnp.int32, rows.shape, 1)
    return jnp.where((lane // HEAD) == head, rows, jnp.zeros_like(rows))


def scores_of(key_ref, query_rows, lo, hi):
    diag = dot(key_ref[lo:hi, :], query_rows, DOT_NT)
    key_pos = lax.broadcasted_iota(jnp.int32, diag.shape, 0)
    query_pos = lax.broadcasted_iota(jnp.int32, diag.shape, 1)
    diag = jnp.where(key_pos <= query_pos, diag, -1e30)
    if lo == 0:
        return diag
    return jnp.concatenate([dot(key_ref[:lo, :], query_rows, DOT_NT), diag], axis=0)


def attend_forward_kernel(q_ref, k_ref, v_ref, o_ref, lse_ref, vt_ref):
    vt_ref[...] = v_ref[...].astype(f32).T.astype(bf16)
    for index in range(LEN // BLOCK_Q):
        lo, hi = index * BLOCK_Q, (index + 1) * BLOCK_Q
        query_rows = q_ref[lo:hi, :] * jnp.asarray(0.125, bf16)
        mixed = []
        for head in range(2):
            scores = scores_of(k_ref, head_rows(query_rows, head), lo, hi)
            highest = jnp.max(scores, axis=0, keepdims=True)
            raised = jnp.exp(scores - highest)
            totals = jnp.sum(raised, axis=0, keepdims=True)
            probabilities = (raised * (1.0 / totals)).astype(bf16)
            mixed.append(dot(vt_ref[head * HEAD : (head + 1) * HEAD, :hi], probabilities, DOT_NN))
            lse_ref[0, head : head + 1, lo:hi] = highest + jnp.log(totals)
        o_ref[lo:hi, :] = jnp.concatenate(mixed, axis=0).T.astype(bf16)


def attend_backward_kernel(q_ref, k_ref, v_ref, lse_ref, do_ref, dq_ref, dk_ref, dv_ref, kt_ref, dk_acc, dv_acc):
    kt_ref[...] = k_ref[...].astype(f32).T.astype(bf16)
    blocks = LEN // BLOCK_Q
    for index in reversed(range(blocks)):
        lo, hi = index * BLOCK_Q, (index + 1) * BLOCK_Q
        query_rows = q_ref[lo:hi, :] * jnp.asarray(0.125, bf16)
        grad_rows = do_ref[lo:hi, :]
        probs, grads, queries, douts, dqs = [], [], [], [], []
        for head in range(2):
            query_head = head_rows(query_rows, head)
            grad_head = head_rows(grad_rows, head)
            scores = scores_of(k_ref, query_head, lo, hi)
            probabilities = jnp.exp(scores - lse_ref[0, head : head + 1, lo:hi])
            grad_probs = dot(v_ref[:hi, :], grad_head, DOT_NT)
            centre = jnp.sum(probabilities * grad_probs, axis=0, keepdims=True)
            grad_scores = (probabilities * (grad_probs - centre)).astype(bf16)
            dqs.append(dot(kt_ref[head * HEAD : (head + 1) * HEAD, :hi], grad_scores, DOT_NN))
            probs.append(probabilities.astype(bf16))
            grads.append(grad_scores)
            queries.append(query_head)
            douts.append(grad_head)
        dq_ref[lo:hi, :] = (0.125 * jnp.concatenate(dqs, axis=0).T).astype(bf16)
        dk = dot(jnp.concatenate(grads, axis=1), jnp.concatenate(queries, axis=0), DOT_NN)
        dv = dot(jnp.concatenate(probs, axis=1), jnp.concatenate(douts, axis=0), DOT_NN)
        if index == blocks - 1:
            dk_acc[...] = dk
            dv_acc[...] = dv
        else:
            dk_acc[:hi, :] = dk_acc[:hi, :] + dk
            dv_acc[:hi, :] = dv_acc[:hi, :] + dv
    dk_ref[...] = dk_acc[...].astype(bf16)
    dv_ref[...] = dv_acc[...].astype(bf16)


def attend_forward(queries, key_rows, value_rows):
    rows, cols = queries.shape
    seqs, pairs = rows // LEN, cols // PAIR
    spec = pl.BlockSpec((LEN, PAIR), lambda s, p: (s, p))
    return pl.pallas_call(
        attend_forward_kernel,
        grid=(seqs, pairs),
        in_specs=[spec] * 3,
        out_specs=[spec, pl.BlockSpec((1, 2, LEN), lambda s, p: (s * pairs + p, 0, 0))],
        out_shape=[
            jax.ShapeDtypeStruct((rows, cols), bf16),
            jax.ShapeDtypeStruct((seqs * pairs, 2, LEN), f32),
        ],
        scratch_shapes=[pltpu.VMEM((PAIR, LEN), bf16)],
        name="attend_forward",
    )(queries, key_rows, value_rows)


def attend_backward(queries, key_rows, value_rows, log_totals, grad_mixed):
    rows, cols = queries.shape
    seqs, pairs = rows // LEN, cols // PAIR
    spec = pl.BlockSpec((LEN, PAIR), lambda s, p: (s, p))
    lse_spec = pl.BlockSpec((1, 2, LEN), lambda s, p: (s * pairs + p, 0, 0))
    return pl.pallas_call(
        attend_backward_kernel,
        grid=(seqs, pairs),
        in_specs=[spec, spec, spec, lse_spec, spec],
        out_specs=[spec] * 3,
        out_shape=[jax.ShapeDtypeStruct((rows, cols), bf16)] * 3,
        scratch_shapes=[
            pltpu.VMEM((PAIR, LEN), bf16),
            pltpu.VMEM((LEN, PAIR), f32),
            pltpu.VMEM((LEN, PAIR), f32),
        ],
        name="attend_backward",
    )(queries, key_rows, value_rows, log_totals, grad_mixed)


GELU_C = 0.7978845608028654


def hidden_kernel(scale_a, ha_ref, hb_ref, dz_ref, wfc_ref, bias_ref, wproj_ref, fa_ref, fb_ref, dua_ref, dub_ref, sa_ref, sb_ref):
    grad_active = dot(dz_ref[...], wproj_ref[...], DOT_NT)
    for h_ref, f_ref, du_ref, s_ref, scale in (
        (ha_ref, fa_ref, dua_ref, sa_ref, scale_a),
        (hb_ref, fb_ref, dub_ref, sb_ref, 1.0),
    ):
        hidden = dot(h_ref[...], wfc_ref[...], DOT_NN) + bias_ref[...]
        square = hidden * hidden
        bend = jnp.tanh(GELU_C * (hidden + 0.044715 * (hidden * square)))
        cdf = 0.5 * (1.0 + bend)
        f_ref[...] = (hidden * cdf).astype(bf16)
        slope = cdf + hidden * (0.5 * (1.0 - bend * bend)) * (
            GELU_C * (1.0 + (3 * 0.044715) * square)
        )
        grad = ((scale * grad_active) * slope).astype(bf16)
        du_ref[...] = grad
        s_ref[0] = jnp.sum(grad.astype(f32), axis=0, keepdims=True)


def hidden_layer(scale_a, h_a, h_b, dz, w_fc, fc_bias, w_proj):
    rows, width = h_a.shape
    hidden = w_fc.shape[1]
    tile_r = min(512, rows)
    tile_c = min(512, hidden)
    row_spec = pl.BlockSpec((tile_r, width), lambda r, c: (r, 0))
    out_spec = pl.BlockSpec((tile_r, tile_c), lambda r, c: (r, c))
    sum_spec = pl.BlockSpec((1, 1, tile_c), lambda r, c: (r, 0, c))
    out = jax.ShapeDtypeStruct((rows, hidden), bf16)
    sums = jax.ShapeDtypeStruct((rows // tile_r, 1, hidden), f32)
    return pl.pallas_call(
        partial(hidden_kernel, scale_a),
        grid=(rows // tile_r, hidden // tile_c),
        in_specs=[
            row_spec,
            row_spec,
            row_spec,
            pl.BlockSpec((width, tile_c), lambda r, c: (0, c)),
            pl.BlockSpec((1, tile_c), lambda r, c: (0, c)),
            pl.BlockSpec((tile_c, width), lambda r, c: (c, 0)),
        ],
        out_specs=[out_spec] * 4 + [sum_spec] * 2,
        out_shape=[out] * 4 + [sums] * 2,
        name="hidden_layer",
    )(h_a, h_b, dz, w_fc, fc_bias.reshape(1, hidden), w_proj)


def norm_parts(values):
    centre = values - jnp.mean(values, axis=-1, keepdims=True)
    spread = jnp.mean(centre * centre, axis=-1, keepdims=True)
    inverse = lax.rsqrt(spread + 1e-05)
    return centre * inverse, inverse


def norm_back(unit, inverse, gain, grad):
    scaled = grad * gain
    along = jnp.mean(scaled * unit, axis=-1, keepdims=True)
    return inverse * (scaled - jnp.mean(scaled, axis=-1, keepdims=True) - unit * along)


def solution(mesh):
    tensor = mesh.shape["tensor"]
    devices_dp = mesh.shape["dp"]
    swap = [(0, 1), (1, 0)]

    def own_rows(values, rows, other=False):
        place = lax.axis_index("tensor")
        if other:
            place = 1 - place
        return lax.dynamic_slice_in_dim(values, place * rows, rows, axis=0)

    def gather_rows(values):
        if tensor != 2:
            return lax.all_gather(values, "tensor", axis=0, tiled=True)
        there = lax.ppermute(values, "tensor", swap)
        first = lax.axis_index("tensor") == 0
        return jnp.concatenate(
            [jnp.where(first, values, there), jnp.where(first, there, values)], axis=0
        )

    def total_rows(shares):
        if tensor != 2:
            return lax.psum(shares.astype(bf16), "tensor").astype(f32)
        there = lax.ppermute(shares.astype(bf16), "tensor", swap)
        return shares + there.astype(f32)

    def scatter_rows(shares, rows):
        if tensor != 2:
            low = shares.astype(bf16)
            return lax.psum_scatter(low, "tensor", scatter_dimension=0, tiled=True).astype(f32)
        low = shares.astype(bf16)
        there = lax.ppermute(own_rows(low, rows, other=True), "tensor", swap)
        return own_rows(low, rows).astype(f32) + there.astype(f32)

    cube = devices_dp == 16

    def flip(values, bit):
        return lax.ppermute(values, "dp", [(index, index ^ bit) for index in range(devices_dp)])

    def side(bit):
        return (lax.axis_index("dp") // bit) % 2

    def half_of(values, which):
        rows = values.shape[0] // 2
        return lax.dynamic_slice_in_dim(values, which * rows, rows, axis=0)

    def halve(values, bit):
        there = flip(half_of(values, 1 - side(bit)), bit)
        return (half_of(values, side(bit)).astype(f32) + there.astype(f32)).astype(bf16)

    def double(values, bit):
        there = flip(values, bit)
        first = side(bit) == 0
        return jnp.concatenate(
            [jnp.where(first, values, there), jnp.where(first, there, values)], axis=0
        )

    def reduce_pair(share_a, share_b):
        shape = share_a.shape
        share_a = share_a.astype(bf16).reshape(shape[0], -1)
        share_b = share_b.astype(bf16).reshape(shape[0], -1)
        if not cube:
            totals = [
                lax.all_gather(
                    lax.psum_scatter(share, "dp", scatter_dimension=0, tiled=True),
                    "dp",
                    axis=0,
                    tiled=True,
                )
                for share in (share_a, share_b)
            ]
            return jnp.stack(totals).astype(f32)
        even = side(1) == 0
        there = flip(jnp.where(even, share_b, share_a), 1)
        kept = jnp.where(even, share_a, share_b)
        mine = (kept.astype(f32) + there.astype(f32)).astype(bf16)
        upper, lower = jnp.split(mine, 2, axis=0)
        upper, lower = halve(upper, 2), halve(lower, 4)
        upper, lower = halve(upper, 4), halve(lower, 2)
        upper, lower = halve(upper, 8), halve(lower, 8)
        upper, lower = double(upper, 8), double(lower, 8)
        upper, lower = double(upper, 4), double(lower, 2)
        upper, lower = double(upper, 2), double(lower, 4)
        mine = jnp.concatenate([upper, lower], axis=0)
        there = flip(mine, 1)
        return jnp.stack([jnp.where(even, mine, there), jnp.where(even, there, mine)]).astype(f32)

    def per_device(
        tokens,
        cotangent,
        gain_one,
        bias_one,
        w_qkv,
        bias_qv,
        w_out,
        out_bias,
        gain_two,
        bias_two,
        w_fc,
        fc_bias,
        w_proj,
        proj_bias,
    ):
        own, width = tokens.shape
        rows = own * tensor
        cols = w_qkv.shape[2]
        hidden_cols = w_fc.shape[1]
        scale_a = float(DEPTH_A) ** (-0.5)
        scale_b = float(DEPTH_B) ** (-0.5)
        factor = 2.0
        assert scale_a == factor * scale_b

        residual = gather_rows(tokens).astype(f32)
        upstream_low = gather_rows(cotangent)
        upstream = upstream_low.astype(f32)
        unit_one, inverse_one = norm_parts(residual)
        normed = (unit_one * gain_one + bias_one).astype(bf16)
        flat_w = w_qkv.reshape(width, 3 * cols)
        projected = dot(normed, flat_w, DOT_NN)
        queries = (projected[:, :cols] + bias_qv[0]).astype(bf16)
        key_rows = projected[:, cols : 2 * cols].astype(bf16)
        value_rows = (projected[:, 2 * cols :] + bias_qv[1]).astype(bf16)
        mixed, log_totals = attend_forward(queries, key_rows, value_rows)
        branch = total_rows(dot(mixed, w_out, DOT_NN)) + out_bias

        dz = (scale_b * upstream).astype(bf16)
        dz_own = (scale_b * cotangent.astype(f32)).astype(bf16)
        proj_sum = jnp.sum(dz_own.astype(f32), axis=0)

        middles, units, inverses, normed_two = [], [], [], []
        for scale in (scale_a, scale_b):
            middle = residual + scale * branch
            unit, inverse = norm_parts(middle)
            middles.append(middle)
            units.append(unit)
            inverses.append(inverse)
            normed_two.append((unit * gain_two + bias_two).astype(bf16))
        f_a, f_b, du_a, du_b, sum_a, sum_b = hidden_layer(
            factor, normed_two[0], normed_two[1], dz, w_fc, fc_bias, w_proj
        )

        outputs, grad_tokens, vectors, weights = [], [], [], []
        place = lax.axis_index("tensor")
        for depth, (scale, active, grad_hidden, hidden_sum, times) in enumerate(
            ((scale_a, f_a, du_a, sum_a, factor), (scale_b, f_b, du_b, sum_b, 1.0))
        ):
            grad_two = total_rows(dot(grad_hidden, w_fc, DOT_NT))
            grad_w_proj = times * dot(active, dz, DOT_TN)
            grad_w_fc = dot(normed_two[depth], grad_hidden, DOT_TN)
            second = scatter_rows(dot(active, w_proj, DOT_NN), own) + proj_bias
            outputs.append((own_rows(middles[depth], own) + scale * second).astype(bf16))

            grad_middle = upstream + norm_back(units[depth], inverses[depth], gain_two, grad_two)
            grad_branch = (scale * grad_middle).astype(bf16)
            own_grad_two = own_rows(grad_two, own)
            grad_gain_two = jnp.sum(own_grad_two * own_rows(units[depth], own), axis=0)
            grad_bias_two = jnp.sum(own_grad_two, axis=0)
            grad_out_bias = jnp.sum(own_rows(grad_branch, own).astype(f32), axis=0)

            grad_w_out = dot(mixed, grad_branch, DOT_TN)
            grad_mixed = dot(grad_branch, w_out, DOT_NT).astype(bf16)
            dq, dk, dv = attend_backward(queries, key_rows, value_rows, log_totals, grad_mixed)
            stacked = jnp.concatenate([dq, dk, dv], axis=1)
            grad_bias_qv = jnp.stack(
                [jnp.sum(dq.astype(f32), axis=0), jnp.sum(dv.astype(f32), axis=0)]
            )
            grad_w_qkv = dot(normed, stacked, DOT_TN)
            grad_one_share = dot(stacked, flat_w, DOT_NT)
            grad_gain_one = jnp.sum(grad_one_share * unit_one, axis=0)
            grad_bias_one = jnp.sum(grad_one_share, axis=0)
            grad_one = scatter_rows(grad_one_share, own)
            grad_tokens.append(
                own_rows(grad_middle, own)
                + norm_back(
                    own_rows(unit_one, own), own_rows(inverse_one, own), gain_one, grad_one
                )
            )
            weights.append((grad_w_qkv, grad_w_out, grad_w_fc, grad_w_proj))
            slots = jnp.concatenate(
                [jnp.sum(hidden_sum, axis=(0, 1)), grad_bias_qv[0], grad_bias_qv[1]]
            )
            spread_slots = jnp.where(
                jnp.arange(tensor)[:, None] == place, slots[None, :], 0.0
            ).reshape(-1)
            vectors.append(
                jnp.concatenate(
                    [
                        grad_gain_one,
                        grad_bias_one,
                        grad_out_bias,
                        grad_gain_two,
                        grad_bias_two,
                        times * proj_sum,
                        spread_slots,
                    ]
                )
            )

        summed = lax.psum(jnp.stack(vectors), ("dp", "tensor"))
        small = [summed[:, index * width : (index + 1) * width] for index in range(6)]
        slot_len = hidden_cols + 2 * cols
        mine = lax.dynamic_slice_in_dim(summed, 6 * width + place * slot_len, slot_len, axis=1)
        grad_fc_bias = mine[:, :hidden_cols]
        grad_bias_qv = mine[:, hidden_cols:].reshape(2, 2, cols)
        stack = [reduce_pair(weights[0][index], weights[1][index]) for index in range(4)]
        return (
            jnp.stack(outputs),
            jnp.stack(grad_tokens),
            small[0],
            small[1],
            stack[0].reshape(2, width, 3, cols),
            grad_bias_qv,
            stack[1],
            small[2],
            small[3],
            small[4],
            stack[2],
            grad_fc_bias,
            stack[3],
            small[5],
        )

    return jax.shard_map(
        per_device,
        mesh=mesh,
        in_specs=(
            P(("dp", "tensor"), None),
            P(("dp", "tensor"), None),
            P(),
            P(),
            P(None, None, "tensor"),
            P(None, "tensor"),
            P("tensor", None),
            P(),
            P(),
            P(),
            P(None, "tensor"),
            P("tensor"),
            P("tensor", None),
            P(),
        ),
        out_specs=(
            P(None, ("dp", "tensor"), None),
            P(None, ("dp", "tensor"), None),
            P(),
            P(),
            P(None, None, None, "tensor"),
            P(None, None, "tensor"),
            P(None, "tensor", None),
            P(),
            P(),
            P(),
            P(None, None, "tensor"),
            P(None, "tensor"),
            P(None, "tensor", None),
            P(),
        ),
        check_vma=False,
    )
```

```python
import jax
import jax.numpy as jnp
from jax import lax
from jax.experimental import pallas as pl
from jax.experimental.pallas import tpu as pltpu
from jax.sharding import PartitionSpec as P

HEAD = 64
LEN = 1024
DEPTH_A = 12
DEPTH_B = 48
PAIR = 2 * HEAD
BLOCK_Q = 256
bf16 = jnp.bfloat16
f32 = jnp.float32

DOT_NT = (((1,), (1,)), ((), ()))
DOT_NN = (((1,), (0,)), ((), ()))
DOT_TN = (((0,), (0,)), ((), ()))


def dot(left, right, dims):
    return lax.dot_general(left, right, dims, preferred_element_type=f32)


def head_rows(rows, head):
    lane = lax.broadcasted_iota(jnp.int32, rows.shape, 1)
    return jnp.where((lane // HEAD) == head, rows, jnp.zeros_like(rows))


def scores_of(key_ref, query_rows, lo, hi):
    diag = dot(key_ref[lo:hi, :], query_rows, DOT_NT)
    key_pos = lax.broadcasted_iota(jnp.int32, diag.shape, 0)
    query_pos = lax.broadcasted_iota(jnp.int32, diag.shape, 1)
    diag = jnp.where(key_pos <= query_pos, diag, -1e30)
    if lo == 0:
        return diag
    return jnp.concatenate([dot(key_ref[:lo, :], query_rows, DOT_NT), diag], axis=0)


def attend_forward_kernel(q_ref, k_ref, v_ref, o_ref, lse_ref, vt_ref):
    vt_ref[...] = v_ref[...].astype(f32).T.astype(bf16)
    for index in range(LEN // BLOCK_Q):
        lo, hi = index * BLOCK_Q, (index + 1) * BLOCK_Q
        query_rows = q_ref[lo:hi, :] * jnp.asarray(0.125, bf16)
        mixed = []
        for head in range(2):
            scores = scores_of(k_ref, head_rows(query_rows, head), lo, hi)
            highest = jnp.max(scores, axis=0, keepdims=True)
            raised = jnp.exp(scores - highest)
            totals = jnp.sum(raised, axis=0, keepdims=True)
            probabilities = (raised * (1.0 / totals)).astype(bf16)
            mixed.append(dot(vt_ref[head * HEAD : (head + 1) * HEAD, :hi], probabilities, DOT_NN))
            lse_ref[0, head : head + 1, lo:hi] = highest + jnp.log(totals)
        o_ref[lo:hi, :] = jnp.concatenate(mixed, axis=0).T.astype(bf16)


def attend_backward_kernel(q_ref, k_ref, v_ref, lse_ref, do_ref, dq_ref, dk_ref, dv_ref, kt_ref, dk_acc, dv_acc):
    kt_ref[...] = k_ref[...].astype(f32).T.astype(bf16)
    blocks = LEN // BLOCK_Q
    for index in reversed(range(blocks)):
        lo, hi = index * BLOCK_Q, (index + 1) * BLOCK_Q
        query_rows = q_ref[lo:hi, :] * jnp.asarray(0.125, bf16)
        grad_rows = do_ref[lo:hi, :]
        probs, grads, queries, douts, dqs = [], [], [], [], []
        for head in range(2):
            query_head = head_rows(query_rows, head)
            grad_head = head_rows(grad_rows, head)
            scores = scores_of(k_ref, query_head, lo, hi)
            probabilities = jnp.exp(scores - lse_ref[0, head : head + 1, lo:hi])
            grad_probs = dot(v_ref[:hi, :], grad_head, DOT_NT)
            centre = jnp.sum(probabilities * grad_probs, axis=0, keepdims=True)
            grad_scores = (probabilities * (grad_probs - centre)).astype(bf16)
            dqs.append(dot(kt_ref[head * HEAD : (head + 1) * HEAD, :hi], grad_scores, DOT_NN))
            probs.append(probabilities.astype(bf16))
            grads.append(grad_scores)
            queries.append(query_head)
            douts.append(grad_head)
        dq_ref[lo:hi, :] = (0.125 * jnp.concatenate(dqs, axis=0).T).astype(bf16)
        dk = dot(jnp.concatenate(grads, axis=1), jnp.concatenate(queries, axis=0), DOT_NN)
        dv = dot(jnp.concatenate(probs, axis=1), jnp.concatenate(douts, axis=0), DOT_NN)
        if index == blocks - 1:
            dk_acc[...] = dk
            dv_acc[...] = dv
        else:
            dk_acc[:hi, :] = dk_acc[:hi, :] + dk
            dv_acc[:hi, :] = dv_acc[:hi, :] + dv
    dk_ref[...] = dk_acc[...].astype(bf16)
    dv_ref[...] = dv_acc[...].astype(bf16)


def attend_forward(queries, key_rows, value_rows):
    rows, cols = queries.shape
    seqs, pairs = rows // LEN, cols // PAIR
    spec = pl.BlockSpec((LEN, PAIR), lambda s, p: (s, p))
    return pl.pallas_call(
        attend_forward_kernel,
        grid=(seqs, pairs),
        in_specs=[spec] * 3,
        out_specs=[spec, pl.BlockSpec((1, 2, LEN), lambda s, p: (s * pairs + p, 0, 0))],
        out_shape=[
            jax.ShapeDtypeStruct((rows, cols), bf16),
            jax.ShapeDtypeStruct((seqs * pairs, 2, LEN), f32),
        ],
        scratch_shapes=[pltpu.VMEM((PAIR, LEN), bf16)],
        name="attend_forward",
    )(queries, key_rows, value_rows)


def attend_backward(queries, key_rows, value_rows, log_totals, grad_mixed):
    rows, cols = queries.shape
    seqs, pairs = rows // LEN, cols // PAIR
    spec = pl.BlockSpec((LEN, PAIR), lambda s, p: (s, p))
    lse_spec = pl.BlockSpec((1, 2, LEN), lambda s, p: (s * pairs + p, 0, 0))
    return pl.pallas_call(
        attend_backward_kernel,
        grid=(seqs, pairs),
        in_specs=[spec, spec, spec, lse_spec, spec],
        out_specs=[spec] * 3,
        out_shape=[jax.ShapeDtypeStruct((rows, cols), bf16)] * 3,
        scratch_shapes=[
            pltpu.VMEM((PAIR, LEN), bf16),
            pltpu.VMEM((LEN, PAIR), f32),
            pltpu.VMEM((LEN, PAIR), f32),
        ],
        name="attend_backward",
    )(queries, key_rows, value_rows, log_totals, grad_mixed)


GELU_C = 0.7978845608028654


def hidden_kernel(scale_ref, ha_ref, hb_ref, dz_ref, wfc_ref, bias_ref, wproj_ref, fa_ref, fb_ref, dua_ref, dub_ref, sa_ref, sb_ref):
    grad_active = dot(dz_ref[...], wproj_ref[...], DOT_NT)
    for h_ref, f_ref, du_ref, s_ref, scale in (
        (ha_ref, fa_ref, dua_ref, sa_ref, scale_ref[0]),
        (hb_ref, fb_ref, dub_ref, sb_ref, scale_ref[1]),
    ):
        hidden = dot(h_ref[...], wfc_ref[...], DOT_NN) + bias_ref[...]
        square = hidden * hidden
        bend = jnp.tanh(GELU_C * (hidden + 0.044715 * (hidden * square)))
        cdf = 0.5 * (1.0 + bend)
        f_ref[...] = (hidden * cdf).astype(bf16)
        slope = cdf + hidden * (0.5 * (1.0 - bend * bend)) * (
            GELU_C * (1.0 + (3 * 0.044715) * square)
        )
        grad = ((scale * grad_active) * slope).astype(bf16)
        du_ref[...] = grad
        s_ref[0] = jnp.sum(grad.astype(f32), axis=0, keepdims=True)


def hidden_layer(scales, h_a, h_b, dz, w_fc, fc_bias, w_proj):
    rows, width = h_a.shape
    hidden = w_fc.shape[1]
    tile_r = min(512, rows)
    tile_c = min(512, hidden)
    row_spec = pl.BlockSpec((tile_r, width), lambda r, c: (r, 0))
    out_spec = pl.BlockSpec((tile_r, tile_c), lambda r, c: (r, c))
    sum_spec = pl.BlockSpec((1, 1, tile_c), lambda r, c: (r, 0, c))
    out = jax.ShapeDtypeStruct((rows, hidden), bf16)
    sums = jax.ShapeDtypeStruct((rows // tile_r, 1, hidden), f32)
    return pl.pallas_call(
        hidden_kernel,
        grid=(rows // tile_r, hidden // tile_c),
        in_specs=[
            pl.BlockSpec(memory_space=pltpu.SMEM),
            row_spec,
            row_spec,
            row_spec,
            pl.BlockSpec((width, tile_c), lambda r, c: (0, c)),
            pl.BlockSpec((1, tile_c), lambda r, c: (0, c)),
            pl.BlockSpec((tile_c, width), lambda r, c: (c, 0)),
        ],
        out_specs=[out_spec] * 4 + [sum_spec] * 2,
        out_shape=[out] * 4 + [sums] * 2,
        name="hidden_layer",
    )(scales, h_a, h_b, dz, w_fc, fc_bias.reshape(1, hidden), w_proj)


def norm_parts(values):
    centre = values - jnp.mean(values, axis=-1, keepdims=True)
    spread = jnp.mean(centre * centre, axis=-1, keepdims=True)
    inverse = lax.rsqrt(spread + 1e-05)
    return centre * inverse, inverse


def norm_back(unit, inverse, gain, grad):
    scaled = grad * gain
    along = jnp.mean(scaled * unit, axis=-1, keepdims=True)
    return inverse * (scaled - jnp.mean(scaled, axis=-1, keepdims=True) - unit * along)


def fence(*values):
    return lax.optimization_barrier(values)


def solution(mesh):
    tensor = mesh.shape["tensor"]
    devices_dp = mesh.shape["dp"]
    cube = devices_dp == 16 and tensor == 2


    def swap(values):
        return lax.ppermute(values, "tensor", [(0, 1), (1, 0)])

    def own_rows(values, rows, other=False):
        place = lax.axis_index("tensor")
        if other:
            place = 1 - place
        return lax.dynamic_slice_in_dim(values, place * rows, rows, axis=0)

    def in_order(values, there):
        first = lax.axis_index("tensor") == 0
        return jnp.concatenate(
            [jnp.where(first, values, there), jnp.where(first, there, values)], axis=0
        )


    def flip(values, bit):
        return lax.ppermute(values, "dp", [(index, index ^ bit) for index in range(devices_dp)])

    def side(bit):
        return (lax.axis_index("dp") // bit) % 2

    def half_of(values, which):
        rows = values.shape[0] // 2
        return lax.dynamic_slice_in_dim(values, which * rows, rows, axis=0)

    def added(values, there):
        return (values.astype(f32) + there.astype(f32)).astype(bf16)

    def joined(values, there, bit):
        first = side(bit) == 0
        return jnp.concatenate(
            [jnp.where(first, values, there), jnp.where(first, there, values)], axis=0
        )

    def reduce_steps(kept, sent):
        (there,) = yield [flip(sent, 1)]
        upper, lower = jnp.split(added(kept, there), 2, axis=0)
        for first, second in ((2, 4), (4, 2), (8, 8)):
            upper_there, lower_there = yield [
                flip(half_of(upper, 1 - side(first)), first),
                flip(half_of(lower, 1 - side(second)), second),
            ]
            upper = added(half_of(upper, side(first)), upper_there)
            lower = added(half_of(lower, side(second)), lower_there)
        for first, second in ((8, 8), (4, 2), (2, 4)):
            upper_there, lower_there = yield [flip(upper, first), flip(lower, second)]
            upper = joined(upper, upper_there, first)
            lower = joined(lower, lower_there, second)
        mine = jnp.concatenate([upper, lower], axis=0)
        (there,) = yield [flip(mine, 1)]
        return mine, there

    def vector_steps(vectors, shared):
        for bit in (1, 2, 4, 8):
            (there,) = yield [flip(vectors, bit)]
            vectors = vectors + there
        (there,) = yield [swap(vectors[:, :shared])]
        return jnp.concatenate([vectors[:, :shared] + there, vectors[:, shared:]], axis=1)

    class Run:
        def __init__(self, steps):
            self.steps = steps
            self.flight = next(steps)

        def feed(self, arrived):
            try:
                self.flight = self.steps.send(arrived)
            except StopIteration as stop:
                self.flight = []
                self.result = stop.value

        def finish(self):
            while self.flight:
                self.feed(self.flight)
            return self.result

    def advance(runs, *values):
        flights = [run.flight for run in runs]
        flat = [item for flight in flights for item in flight]
        held = fence(*flat, *values)
        place = 0
        for run, flight in zip(runs, flights):
            run.feed(list(held[place : place + len(flight)]))
            place += len(flight)
        rest = held[place:]
        return rest[0] if len(rest) == 1 else rest

    def per_device(
        tokens,
        cotangent,
        gain_one,
        bias_one,
        w_qkv,
        bias_qv,
        w_out,
        out_bias,
        gain_two,
        bias_two,
        w_fc,
        fc_bias,
        w_proj,
        proj_bias,
    ):
        own, width = tokens.shape
        rows = own * tensor
        cols = w_qkv.shape[2]
        hidden_cols = w_fc.shape[1]
        scale_a = float(DEPTH_A) ** (-0.5)
        scale_b = float(DEPTH_B) ** (-0.5)
        factor = 2.0
        assert scale_a == factor * scale_b
        even = side(1) == 0 if cube else jnp.asarray(True)
        scales = [jnp.where(even, scale_a, scale_b), jnp.where(even, scale_b, scale_a)]
        times = jnp.where(even, jnp.array([factor, 1.0], f32), jnp.array([1.0, factor], f32))

        def by_depth(kept, sent):
            return jnp.stack([jnp.where(even, kept, sent), jnp.where(even, sent, kept)])

        if cube:
            there, cotangent = fence(swap(tokens), cotangent)
            residual = in_order(tokens, there).astype(f32)
            cotangent_there = swap(cotangent)
        else:
            residual = lax.all_gather(tokens, "tensor", axis=0, tiled=True).astype(f32)
        unit_one, inverse_one = norm_parts(residual)
        normed = (unit_one * gain_one + bias_one).astype(bf16)
        flat_w = w_qkv.reshape(width, 3 * cols)
        projected = dot(normed, flat_w, DOT_NN)
        queries = (projected[:, :cols] + bias_qv[0]).astype(bf16)
        key_rows = projected[:, cols : 2 * cols].astype(bf16)
        value_rows = (projected[:, 2 * cols :] + bias_qv[1]).astype(bf16)
        mixed, log_totals = attend_forward(queries, key_rows, value_rows)
        if cube:
            mixed, cotangent_there = fence(mixed, cotangent_there)
            upstream = in_order(cotangent, cotangent_there).astype(f32)
        else:
            upstream = lax.all_gather(cotangent, "tensor", axis=0, tiled=True).astype(f32)
        branch_share = dot(mixed, w_out, DOT_NN)
        if cube:
            branch = branch_share + swap(branch_share.astype(bf16)).astype(f32) + out_bias
        else:
            branch = lax.psum(branch_share.astype(bf16), "tensor").astype(f32) + out_bias

        dz = (scale_b * upstream).astype(bf16)
        proj_sum = jnp.sum((scale_b * cotangent.astype(f32)).astype(bf16).astype(f32), axis=0)

        middles, units, inverses, normed_two = [], [], [], []
        for scale in scales:
            middle = residual + scale * branch
            unit, inverse = norm_parts(middle)
            middles.append(middle)
            units.append(unit)
            inverses.append(inverse)
            normed_two.append((unit * gain_two + bias_two).astype(bf16))
        f_0, f_1, du_0, du_1, sum_0, sum_1 = hidden_layer(
            times, normed_two[0], normed_two[1], dz, w_fc, fc_bias, w_proj
        )
        actives, grad_hiddens = [f_0, f_1], [du_0, du_1]

        def second_norm_back(depth, grad_two):
            grad_middle = upstream + norm_back(units[depth], inverses[depth], gain_two, grad_two)
            grad_branch = (scales[depth] * grad_middle).astype(bf16)
            own_grad = own_rows(grad_two, own)
            sums = [
                jnp.sum(own_rows(grad_branch, own).astype(f32), axis=0),
                jnp.sum(own_grad * own_rows(units[depth], own), axis=0),
                jnp.sum(own_grad, axis=0),
            ]
            grad_w_out = dot(mixed, grad_branch, DOT_TN).astype(bf16)
            grad_mixed = dot(grad_branch, w_out, DOT_NT).astype(bf16)
            return grad_middle, sums, grad_w_out, grad_mixed

        def attention_back(grad_mixed):
            return attend_backward(queries, key_rows, value_rows, log_totals, grad_mixed)

        def projection_back(dq, dk, dv):
            stacked = jnp.concatenate([dq, dk, dv], axis=1)
            bias_sums = [jnp.sum(dq.astype(f32), axis=0), jnp.sum(dv.astype(f32), axis=0)]
            grad_w_qkv = dot(normed, stacked, DOT_TN).astype(bf16)
            share = dot(stacked, flat_w, DOT_NT)
            sums = [jnp.sum(share * unit_one, axis=0), jnp.sum(share, axis=0)]
            return bias_sums, grad_w_qkv, share, sums

        def grad_proj(depth):
            return (times[depth] * dot(actives[depth], dz, DOT_TN)).astype(bf16)

        def grad_fc(depth):
            return dot(normed_two[depth], grad_hiddens[depth], DOT_TN).astype(bf16)

        def grad_two_share(depth):
            return dot(grad_hiddens[depth], w_fc, DOT_NT)

        def second_share(depth):
            return dot(actives[depth], w_proj, DOT_NN).astype(bf16)

        grads_out, grads_qkv, outputs, grad_inputs = [None] * 2, [None] * 2, [], []
        middle_grads, sums_two, sums_one, bias_sums = [None] * 2, [None] * 2, [None] * 2, [None] * 2
        if cube:
            share_0 = grad_two_share(0)
            share_1 = grad_two_share(1)
            low_1 = share_1.astype(bf16)
            cross_0 = swap(share_0.astype(bf16))
            proj_sent = grad_proj(1)
            run_proj = Run(reduce_steps(grad_proj(0), proj_sent))
            fc_kept, fc_sent = grad_fc(0), grad_fc(1)
            fc_kept, fc_sent = advance([run_proj], fc_kept, fc_sent)
            run_fc = Run(reduce_steps(fc_kept, fc_sent))
            seconds = [second_share(0), second_share(1)]
            cross_0, low_1, *seconds = advance([run_fc], cross_0, low_1, *seconds)
            cross_1 = swap(low_1)

            grad_two = share_0 + cross_0.astype(f32)
            middle_grads[0], sums_two[0], grads_out[0], grad_mixed = second_norm_back(0, grad_two)
            grad_mixed = advance([run_proj], grad_mixed)
            parts = attention_back(grad_mixed)
            *parts, cross_1 = advance([run_proj, run_fc], *parts, cross_1)
            second_there = [swap(own_rows(item, own, other=True)) for item in seconds]
            bias_sums[0], grads_qkv[0], share_one_0, sums_one[0] = projection_back(*parts)
            grad_two = share_1 + cross_1.astype(f32)
            middle_grads[1], sums_two[1], grads_out[1], grad_mixed = second_norm_back(1, grad_two)
            grad_mixed, *second_there = advance([run_proj, run_fc], grad_mixed, *second_there)
            run_out = Run(reduce_steps(grads_out[0], grads_out[1]))
            one_there = [swap(own_rows(share_one_0, own, other=True).astype(bf16))]
            parts = attention_back(grad_mixed)
            *parts, first_there = advance([run_proj, run_fc, run_out], *parts, one_there[0])
            bias_sums[1], grads_qkv[1], share_one_1, sums_one[1] = projection_back(*parts)
            run_qkv = Run(reduce_steps(grads_qkv[0], grads_qkv[1]))
            one_there = [first_there, swap(own_rows(share_one_1, own, other=True).astype(bf16))]
            shares_one = [share_one_0, share_one_1]
            seconds = [
                own_rows(item, own).astype(f32) + there.astype(f32)
                for item, there in zip(seconds, second_there)
            ]
            grads_one = [
                own_rows(share, own) + there.astype(f32)
                for share, there in zip(shares_one, one_there)
            ]
        else:
            totals = []
            grads_proj = [grad_proj(0), grad_proj(1)]
            grads_fc = [grad_fc(0), grad_fc(1)]
            seconds, grads_one = [], []
            for depth in range(2):
                grad_two = lax.psum(grad_two_share(depth).astype(bf16), "tensor").astype(f32)
                seconds.append(
                    lax.psum_scatter(
                        second_share(depth), "tensor", scatter_dimension=0, tiled=True
                    ).astype(f32)
                )
                middle_grads[depth], sums_two[depth], grads_out[depth], grad_mixed = (
                    second_norm_back(depth, grad_two)
                )
                bias_sums[depth], grads_qkv[depth], share, sums_one[depth] = projection_back(
                    *attention_back(grad_mixed)
                )
                grads_one.append(
                    lax.psum_scatter(
                        share.astype(bf16), "tensor", scatter_dimension=0, tiled=True
                    ).astype(f32)
                )

        vectors = jnp.stack(
            [
                jnp.concatenate(
                    sums_one[depth]
                    + sums_two[depth]
                    + [times[depth] * proj_sum, jnp.sum(hidden_sum, axis=(0, 1))]
                    + bias_sums[depth]
                )
                for depth, hidden_sum in enumerate((sum_0, sum_1))
            ]
        )
        vectors = by_depth(vectors[0], vectors[1])
        shared = 6 * width
        if cube:
            run_vectors = Run(vector_steps(vectors, shared))
            summed = run_vectors.finish()
            stack = [
                by_depth(*run.finish()).astype(f32) for run in (run_proj, run_fc, run_out, run_qkv)
            ]
        else:
            summed = jnp.concatenate(
                [
                    lax.psum(vectors[:, :shared], ("dp", "tensor")),
                    lax.psum(vectors[:, shared:], "dp"),
                ],
                axis=1,
            )
            stack = [
                jnp.stack(
                    [
                        lax.all_gather(
                            lax.psum_scatter(share, "dp", scatter_dimension=0, tiled=True),
                            "dp",
                            axis=0,
                            tiled=True,
                        )
                        for share in pair
                    ]
                ).astype(f32)
                for pair in (grads_proj, grads_fc, grads_out, grads_qkv)
            ]
        grad_w_proj, grad_w_fc, grad_w_out, grad_w_qkv = stack

        for depth in range(2):
            second = seconds[depth] + proj_bias
            outputs.append(
                (own_rows(middles[depth], own) + scales[depth] * second).astype(bf16)
            )
            grad_inputs.append(
                own_rows(middle_grads[depth], own)
                + norm_back(
                    own_rows(unit_one, own), own_rows(inverse_one, own), gain_one, grads_one[depth]
                )
            )
        small = [summed[:, index * width : (index + 1) * width] for index in range(6)]
        rest = summed[:, shared:]
        return (
            by_depth(*outputs),
            by_depth(*grad_inputs),
            small[0],
            small[1],
            grad_w_qkv.reshape(2, width, 3, cols),
            rest[:, hidden_cols:].reshape(2, 2, cols),
            grad_w_out,
            small[2],
            small[3],
            small[4],
            grad_w_fc,
            rest[:, :hidden_cols],
            grad_w_proj,
            small[5],
        )

    return jax.shard_map(
        per_device,
        mesh=mesh,
        in_specs=(
            P(("dp", "tensor"), None),
            P(("dp", "tensor"), None),
            P(),
            P(),
            P(None, None, "tensor"),
            P(None, "tensor"),
            P("tensor", None),
            P(),
            P(),
            P(),
            P(None, "tensor"),
            P("tensor"),
            P("tensor", None),
            P(),
        ),
        out_specs=(
            P(None, ("dp", "tensor"), None),
            P(None, ("dp", "tensor"), None),
            P(),
            P(),
            P(None, None, None, "tensor"),
            P(None, None, "tensor"),
            P(None, "tensor", None),
            P(),
            P(),
            P(),
            P(None, None, "tensor"),
            P(None, "tensor"),
            P(None, "tensor", None),
            P(),
        ),
        check_vma=False,
    )
```
